32 devices in a mesh: users: 16 (over z, x, core), period: 2 (over y).
Axes of the slice: x: 2, y: 2, z: 4, core: 2. Of those that a mesh axis runs over, the one named last changes fastest.
Arguments:
- ratings: float32 [2, 6, 6144, 768], P('period', None, 'users'), may hold values from -6 to 6
- observed: bfloat16 [2, 6, 6144, 768], P('period', None, 'users'), may hold values from 0 to 2, as said below
- user_factors: float32 [6144, 256], P('users'), may hold values from -0.625 to 0.625
- item_factors: float32 [2, 12288, 256], P('period', 'users'), may hold values from -0.625 to 0.625
Outputs:
- user_out: float32 [6144, 256], P('users')
- item_out: float32 [2, 12288, 256], P('period', 'users')
The draws below stay inside these ranges and needn't reach their ends.
Inputs may be any that keep to these rules, and one draw needn't show every extreme that they name: `observed`: an entry is either 0 (unobserved) or a weight of 0.5 or more.
All inputs are finite; a program needn't handle non-finite values.
Results may differ from the reference program's by a relative error of at most 0.0003.
Values sent between devices are 32-bit elements; how exact they have to be, the bound alone decides.
No kernel may reach another device: no remote copies, remote signals or barrier semaphores. Data moves between devices by JAX's collectives and lax.ppermute only.
A program may use at most 64 MiB of HBM per device.

```python
import jax
import jax.numpy as jnp
from jax import lax

R = 256
UB = 384
IB = 768
OUTER = 2
STRATA = 3
NBLOCKS = 16
PERIODS = 2
USERS = 6144
ITEMS = 12288


def draw_observed(key, part):
    entry_shape = (PERIODS, OUTER * STRATA, USERS, IB)
    chance = jax.random.uniform(jax.random.fold_in(key, 11), entry_shape, jnp.float32)
    level = jax.random.uniform(jax.random.fold_in(key, 12), entry_shape, jnp.float32, 0.5, 2.0)
    return jnp.where(chance < 0.6, level, 0.0).astype(jnp.bfloat16)


def shard_levels(rng, dims, split, least, high):
    factor_of = 1.0
    for position, parts in split:
        heights = jax.random.uniform(jax.random.fold_in(jax.random.fold_in(rng, 6), position), (parts,), jnp.float32, least / len(split), high / len(split))
        factor_of = factor_of * jnp.repeat(jnp.exp(heights), dims[position] // parts).reshape((-1,) + (1,) * (len(dims) - 1 - position))
    return factor_of


def gaussian(rng, dims, scale, most, shards=(), dtype=jnp.bfloat16):
    loudness = shard_levels(rng, dims, shards, -0.22, 0.18) if shards else 1.0
    values = jax.random.normal(rng, dims, jnp.float32) * scale * loudness
    return jnp.minimum(jnp.maximum(values, -most), most).astype(dtype)


def setup_inputs(seed: int = 0) -> dict:
    arg_keys = jax.random.split(jax.random.key(seed), 5)
    return {
        "ratings": gaussian(arg_keys[0], (PERIODS, OUTER * STRATA, USERS, IB), 1.0, 6.0, ((0, 2), (2, 16)), jnp.float32),
        "observed": draw_observed(jax.random.fold_in(arg_keys[4], 71), 0),
        "user_factors": gaussian(arg_keys[2], (USERS, R), 0.25, 0.625, ((0, 16),), jnp.float32),
        "item_factors": gaussian(arg_keys[3], (PERIODS, ITEMS, R), 0.25, 0.625, ((0, 2), (1, 16)), jnp.float32),
    }


step_rate = 0.002


def reference(ratings, observed, user_factors, item_factors):
    highest = lax.Precision.HIGHEST
    factors_u = user_factors
    items_all = item_factors
    for outer_step in range(OUTER):
        anchor = factors_u.reshape(NBLOCKS, UB, R)
        summed_change = jnp.zeros((NBLOCKS, UB, R), jnp.float32)
        new_items = []
        for period_p in range(PERIODS):
            current = anchor
            blocks_v = items_all[period_p].reshape(NBLOCKS, IB, R)
            for within in range(STRATA):
                stratum = outer_step * STRATA + within
                paired = jnp.roll(blocks_v, -stratum, axis=0)
                tile_rows = ratings[period_p, stratum].reshape(NBLOCKS, UB, IB)
                weights = observed[period_p, stratum].reshape(NBLOCKS, UB, IB).astype(jnp.float32)
                predicted = jnp.einsum("bur,bir->bui", current, paired, precision=highest)
                residual = weights * (tile_rows - predicted)
                new_u = current + step_rate * jnp.einsum("bui,bir->bur", residual, paired, precision=highest)
                new_v = paired + step_rate * jnp.einsum("bui,bur->bir", residual, current, precision=highest)
                current = new_u
                blocks_v = jnp.roll(new_v, stratum, axis=0)
            summed_change = summed_change + (current - anchor)
            new_items.append(blocks_v.reshape(ITEMS, R))
        factors_u = (anchor + summed_change / PERIODS).reshape(USERS, R)
        items_all = jnp.stack(new_items, axis=0)
    return factors_u, items_all
```

```python
import jax
import jax.numpy as jnp
from jax import lax
from jax.sharding import PartitionSpec as P

OUTER = 2
STRATA = 3
PIECES = 3


step_rate = 0.002


def from_behind(array, axis, by):
    peers = lax.axis_size(axis)
    return lax.ppermute(array, axis, [(i, (i + by) % peers) for i in range(peers)])


def dot(lhs, rhs, dims):
    return lax.dot_general(
        lhs, rhs, (dims, ((), ())), precision=lax.Precision.HIGH, preferred_element_type=jnp.float32
    )


def combine(anchor, current):
    change = current - anchor
    periods_count = lax.axis_size("period")
    if periods_count & (periods_count - 1):
        summed = lax.psum(change, "period")
    else:
        summed, reach = change, 1
        while reach < periods_count:
            partners = [(i, i ^ reach) for i in range(periods_count)]
            summed = summed + lax.ppermute(summed, "period", partners)
            reach *= 2
    return anchor + summed / periods_count


def on_device(ratings, observed, user_factors, item_factors):
    factors_u = user_factors
    items = item_factors.shape[1]
    rows = items // PIECES
    pieces = [item_factors[0, i * rows : (i + 1) * rows] for i in range(PIECES)]
    last = OUTER * STRATA - 1
    for outer_step in range(OUTER):
        anchor = factors_u
        current = factors_u
        for within in range(STRATA):
            stratum = outer_step * STRATA + within
            gained = current
            for i in range(PIECES):
                cols = slice(i * rows, (i + 1) * rows)
                held = pieces[i]
                predicted = dot(current, held, ((1,), (1,)))
                weights = observed[0, stratum, :, cols].astype(jnp.float32)
                residual = weights * (ratings[0, stratum, :, cols] - predicted)
                moved = held + step_rate * dot(residual, current, ((0,), (0,)))
                gained = gained + step_rate * dot(residual, held, ((1,), (0,)))
                pieces[i] = from_behind(moved, "users", last if stratum == last else -1)
            current = gained
        factors_u = combine(anchor, current)
    return (factors_u, jnp.concatenate(pieces, axis=0)[None])


def solution(mesh):
    in_specs = (
        P("period", None, "users", None),
        P("period", None, "users", None),
        P("users", None),
        P("period", "users", None),
    )
    out_specs = (P("users", None), P("period", "users", None))
    return jax.shard_map(
        on_device, mesh=mesh, in_specs=in_specs, out_specs=out_specs, check_vma=False
    )
```

```python
import jax
import jax.numpy as jnp
from jax import lax
from jax.sharding import PartitionSpec as P


OUTER = 2
STRATA = 3
PIECES = 6


step_rate = 0.002


def from_behind(array, axis, by):
    peers = lax.axis_size(axis)
    return lax.ppermute(array, axis, [(i, (i + by) % peers) for i in range(peers)])


def dot(lhs, rhs, dims):
    return lax.dot_general(
        lhs, rhs, (dims, ((), ())), precision=lax.Precision.HIGH, preferred_element_type=jnp.float32
    )


def combine(current):
    periods_count = lax.axis_size("period")
    if periods_count & (periods_count - 1):
        summed = lax.psum(current, "period")
    else:
        summed, reach = current, 1
        while reach < periods_count:
            partners = [(i, i ^ reach) for i in range(periods_count)]
            partner = lax.ppermute(summed, "period", partners)
            summed = summed + partner
            reach *= 2
    return summed / periods_count


def on_device(ratings, observed, user_factors, item_factors):
    factors_u = user_factors
    items = item_factors.shape[1]
    rows = items // PIECES
    pieces = [item_factors[0, i * rows : (i + 1) * rows] for i in range(PIECES)]
    last = OUTER * STRATA - 1
    for outer_step in range(OUTER):
        current = factors_u
        for within in range(STRATA):
            stratum = outer_step * STRATA + within
            gained = current
            for i in range(PIECES):
                cols = slice(i * rows, (i + 1) * rows)
                held = pieces[i]
                predicted = dot(current, held, ((1,), (1,)))
                weights = observed[0, stratum, :, cols].astype(jnp.float32)
                residual = weights * (ratings[0, stratum, :, cols] - predicted)
                moved = held + step_rate * dot(residual, current, ((0,), (0,)))
                gained = gained + step_rate * dot(residual, held, ((1,), (0,)))
                pieces[i] = from_behind(moved, "users", last if stratum == last else -1)
            current = gained
        factors_u = combine(current)
    return (factors_u, jnp.concatenate(pieces, axis=0)[None])


def solution(mesh):
    in_specs = (
        P("period", None, "users", None),
        P("period", None, "users", None),
        P("users", None),
        P("period", "users", None),
    )
    out_specs = (P("users", None), P("period", "users", None))
    return jax.shard_map(
        on_device, mesh=mesh, in_specs=in_specs, out_specs=out_specs, check_vma=False
    )
```

```python
import functools

import jax
import jax.numpy as jnp
from jax import lax
from jax.experimental import pallas as pl
from jax.experimental.pallas import tpu as pltpu
from jax.sharding import PartitionSpec as P


OUTER = 2
STRATA = 3
PIECES = 3


step_rate = 0.002


def from_behind(array, axis, by):
    peers = lax.axis_size(axis)
    return lax.ppermute(array, axis, [(i, (i + by) % peers) for i in range(peers)])


def dot(lhs, rhs, dims):
    return lax.dot_general(
        lhs, rhs, (dims, ((), ())), precision=lax.Precision.HIGH, preferred_element_type=jnp.float32
    )


def halves(x):
    high = x.astype(jnp.bfloat16)
    return high, (x - high.astype(jnp.float32)).astype(jnp.bfloat16)


def dot_of_halves(lhs, rhs, dims):
    part = functools.partial(
        lax.dot_general, dimension_numbers=(dims, ((), ())), preferred_element_type=jnp.float32
    )
    return part(lhs[0], rhs[0]) + (part(lhs[0], rhs[1]) + part(lhs[1], rhs[0]))


def first_kernel(at, c_hbm, v_hbm, r_hbm, w_hbm, moved_ref, gain_ref, c, v, r, w, sems):
    rows = v.shape[0]
    copies = [
        pltpu.make_async_copy(c_hbm, c, sems.at[0]),
        pltpu.make_async_copy(v_hbm.at[0, pl.ds(at * rows, rows)], v, sems.at[1]),
        pltpu.make_async_copy(r_hbm.at[0, 0, :, pl.ds(at * rows, rows)], r, sems.at[2]),
        pltpu.make_async_copy(w_hbm.at[0, 0, :, pl.ds(at * rows, rows)], w, sems.at[3]),
    ]
    for copy in copies:
        copy.start()
    copies[0].wait()
    copies[1].wait()
    c_halves, v_halves = halves(c[...]), halves(v[...])
    predicted = dot_of_halves(c_halves, v_halves, ((1,), (1,)))
    copies[2].wait()
    copies[3].wait()
    residual = halves(w[...].astype(jnp.float32) * (r[...] - predicted))
    moved_ref[...] = v[...] + step_rate * dot_of_halves(residual, c_halves, ((0,), (0,)))
    gain_ref[...] = step_rate * dot_of_halves(residual, v_halves, ((1,), (0,)))


def first_piece(at, user_factors, item_factors, ratings, observed):
    users, rank = user_factors.shape
    rows = item_factors.shape[1] // PIECES
    anywhere = pl.BlockSpec(memory_space=pltpu.HBM)
    inside = pl.BlockSpec(memory_space=pltpu.VMEM)
    return pl.pallas_call(
        functools.partial(first_kernel, at),
        out_shape=(
            jax.ShapeDtypeStruct((rows, rank), jnp.float32),
            jax.ShapeDtypeStruct((users, rank), jnp.float32),
        ),
        in_specs=[anywhere] * 4,
        out_specs=(inside, inside),
        scratch_shapes=[
            pltpu.VMEM((users, rank), jnp.float32),
            pltpu.VMEM((rows, rank), jnp.float32),
            pltpu.VMEM((users, rows), jnp.float32),
            pltpu.VMEM((users, rows), jnp.bfloat16),
            pltpu.SemaphoreType.DMA((4,)),
        ],
        compiler_params=pltpu.CompilerParams(vmem_limit_bytes=58 << 20),
        cost_estimate=pl.CostEstimate(
            flops=18 * users * rows * rank,
            bytes_accessed=4 * (users * rank + rows * rank) + 6 * users * rows,
            transcendentals=0,
        ),
    )(user_factors, item_factors, ratings, observed)


def combine(current):
    periods_count = lax.axis_size("period")
    if periods_count & (periods_count - 1):
        summed = lax.psum(current, "period")
    else:
        summed, reach = current, 1
        while reach < periods_count:
            partners = [(i, i ^ reach) for i in range(periods_count)]
            partner = lax.ppermute(summed, "period", partners)
            summed = summed + partner
            reach *= 2
    return summed / periods_count


def on_device(ratings, observed, user_factors, item_factors):
    factors_u = user_factors
    items = item_factors.shape[1]
    rows = items // PIECES
    pieces = [None] * PIECES
    last = OUTER * STRATA - 1
    for outer_step in range(OUTER):
        current = factors_u
        for within in range(STRATA):
            stratum = outer_step * STRATA + within
            gained = current
            for i in range(PIECES):
                if stratum == 0:
                    moved, gain = first_piece(i, current, item_factors, ratings, observed)
                    gained = gained + gain
                else:
                    cols = slice(i * rows, (i + 1) * rows)
                    held = pieces[i]
                    predicted = dot(current, held, ((1,), (1,)))
                    weights = observed[0, stratum, :, cols].astype(jnp.float32)
                    residual = weights * (ratings[0, stratum, :, cols] - predicted)
                    moved = held + step_rate * dot(residual, current, ((0,), (0,)))
                    gained = gained + step_rate * dot(residual, held, ((1,), (0,)))
                pieces[i] = from_behind(moved, "users", last if stratum == last else -1)
            current = gained
        factors_u = combine(current)
    return (factors_u, jnp.concatenate(pieces, axis=0)[None])


def solution(mesh):
    in_specs = (
        P("period", None, "users", None),
        P("period", None, "users", None),
        P("users", None),
        P("period", "users", None),
    )
    out_specs = (P("users", None), P("period", "users", None))
    return jax.shard_map(
        on_device, mesh=mesh, in_specs=in_specs, out_specs=out_specs, check_vma=False
    )
```

```python
import jax
import jax.numpy as jnp
from jax import lax
from jax.experimental import pallas as pl
from jax.experimental.pallas import tpu as pltpu
from jax.sharding import PartitionSpec as P


OUTER = 2
STRATA = 3
PIECES = 3


step_rate = 0.002


def from_behind(array, axis, by):
    peers = lax.axis_size(axis)
    return lax.ppermute(array, axis, [(i, (i + by) % peers) for i in range(peers)])


def dot(lhs, rhs, dims):
    return lax.dot_general(
        lhs, rhs, (dims, ((), ())), precision=lax.Precision.HIGH, preferred_element_type=jnp.float32
    )


def load_kernel(c_in, v_in, r_in, w_in, c_out, v_out, r_out, w_out, sems):
    copies = [
        pltpu.make_async_copy(c_in, c_out, sems.at[0]),
        pltpu.make_async_copy(v_in.at[0], v_out, sems.at[1]),
        pltpu.make_async_copy(r_in.at[0, 0], r_out, sems.at[2]),
        pltpu.make_async_copy(w_in.at[0, 0], w_out, sems.at[3]),
    ]
    for copy in copies:
        copy.start()
    for copy in copies:
        copy.wait()


def load_first(user_factors, item_factors, ratings, observed):
    operands = (user_factors, item_factors, ratings, observed)
    shapes = (user_factors.shape, item_factors.shape[1:], ratings.shape[2:], observed.shape[2:])
    return pl.pallas_call(
        load_kernel,
        out_shape=tuple(jax.ShapeDtypeStruct(s, a.dtype) for s, a in zip(shapes, operands)),
        in_specs=[pl.BlockSpec(memory_space=pltpu.HBM)] * 4,
        out_specs=(pl.BlockSpec(memory_space=pltpu.VMEM),) * 4,
        scratch_shapes=[pltpu.SemaphoreType.DMA((4,))],
        compiler_params=pltpu.CompilerParams(vmem_limit_bytes=8 << 20),
    )(*[pltpu.with_memory_space_constraint(a, pltpu.HBM) for a in operands])


def combine(current):
    periods_count = lax.axis_size("period")
    if periods_count & (periods_count - 1):
        summed = lax.psum(current, "period")
    else:
        summed, reach = current, 1
        while reach < periods_count:
            partners = [(i, i ^ reach) for i in range(periods_count)]
            partner = lax.ppermute(summed, "period", partners)
            summed = summed + partner
            reach *= 2
    return summed / periods_count


def on_device(ratings, observed, user_factors, item_factors):
    factors_u, first_items, first_ratings, first_weights = load_first(
        user_factors, item_factors, ratings, observed
    )
    items = item_factors.shape[1]
    rows = items // PIECES
    pieces = [first_items[i * rows : (i + 1) * rows] for i in range(PIECES)]
    last = OUTER * STRATA - 1
    for outer_step in range(OUTER):
        current = factors_u
        for within in range(STRATA):
            stratum = outer_step * STRATA + within
            gained = current
            for i in range(PIECES):
                cols = slice(i * rows, (i + 1) * rows)
                if stratum == 0:
                    tile, weights = first_ratings[:, cols], first_weights[:, cols]
                else:
                    tile, weights = ratings[0, stratum, :, cols], observed[0, stratum, :, cols]
                held = pieces[i]
                predicted = dot(current, held, ((1,), (1,)))
                residual = weights.astype(jnp.float32) * (tile - predicted)
                moved = held + step_rate * dot(residual, current, ((0,), (0,)))
                gained = gained + step_rate * dot(residual, held, ((1,), (0,)))
                pieces[i] = from_behind(moved, "users", last if stratum == last else -1)
            current = gained
        factors_u = combine(current)
    return (factors_u, jnp.concatenate(pieces, axis=0)[None])


def solution(mesh):
    in_specs = (
        P("period", None, "users", None),
        P("period", None, "users", None),
        P("users", None),
        P("period", "users", None),
    )
    out_specs = (P("users", None), P("period", "users", None))
    return jax.shard_map(
        on_device, mesh=mesh, in_specs=in_specs, out_specs=out_specs, check_vma=False
    )
```

```python
import jax
import jax.numpy as jnp
from jax import lax
from jax.experimental import pallas as pl
from jax.experimental.pallas import tpu as pltpu
from jax.sharding import PartitionSpec as P


OUTER = 2
STRATA = 3
PIECES = 3
LAYER = 4
SPLIT_ROUTE = (0,)


step_rate = 0.002


def from_behind(array, axis, by):
    peers = lax.axis_size(axis)
    return lax.ppermute(array, axis, [(i, (i + by) % peers) for i in range(peers)])


def home(array, by, split):
    peers = lax.axis_size("users")
    if not split or peers % LAYER:
        return from_behind(array, "users", by)
    across = [(i, (i + (i % LAYER + by) // LAYER * LAYER) % peers) for i in range(peers)]
    within = [(i, i // LAYER * LAYER + (i + by) % LAYER) for i in range(peers)]
    array = lax.ppermute(array, "users", across)
    return lax.ppermute(array, "users", within)


def dot(lhs, rhs, dims):
    return lax.dot_general(
        lhs, rhs, (dims, ((), ())), precision=lax.Precision.HIGH, preferred_element_type=jnp.float32
    )


def load_kernel(c_in, v_in, r_in, w_in, c_out, v_out, r_out, w_out, sems):
    copies = [
        pltpu.make_async_copy(c_in, c_out, sems.at[0]),
        pltpu.make_async_copy(v_in.at[0], v_out, sems.at[1]),
        pltpu.make_async_copy(r_in.at[0, 0], r_out, sems.at[2]),
        pltpu.make_async_copy(w_in.at[0, 0], w_out, sems.at[3]),
    ]
    for copy in copies:
        copy.start()
    for copy in copies:
        copy.wait()


def load_first(user_factors, item_factors, ratings, observed):
    operands = (user_factors, item_factors, ratings, observed)
    shapes = (user_factors.shape, item_factors.shape[1:], ratings.shape[2:], observed.shape[2:])
    return pl.pallas_call(
        load_kernel,
        out_shape=tuple(jax.ShapeDtypeStruct(s, a.dtype) for s, a in zip(shapes, operands)),
        in_specs=[pl.BlockSpec(memory_space=pltpu.HBM)] * 4,
        out_specs=(pl.BlockSpec(memory_space=pltpu.VMEM),) * 4,
        scratch_shapes=[pltpu.SemaphoreType.DMA((4,))],
        compiler_params=pltpu.CompilerParams(vmem_limit_bytes=8 << 20),
    )(*[pltpu.with_memory_space_constraint(a, pltpu.HBM) for a in operands])


def combine(current):
    periods_count = lax.axis_size("period")
    if periods_count & (periods_count - 1):
        summed = lax.psum(current, "period")
    else:
        summed, reach = current, 1
        while reach < periods_count:
            partners = [(i, i ^ reach) for i in range(periods_count)]
            partner = lax.ppermute(summed, "period", partners)
            summed = summed + partner
            reach *= 2
    return summed / periods_count


def on_device(ratings, observed, user_factors, item_factors):
    factors_u, first_items, first_ratings, first_weights = load_first(
        user_factors, item_factors, ratings, observed
    )
    items = item_factors.shape[1]
    rows = items // PIECES
    pieces = [first_items[i * rows : (i + 1) * rows] for i in range(PIECES)]
    last = OUTER * STRATA - 1
    for outer_step in range(OUTER):
        current = factors_u
        for within in range(STRATA):
            stratum = outer_step * STRATA + within
            gained = current
            for i in range(PIECES):
                cols = slice(i * rows, (i + 1) * rows)
                if stratum == 0:
                    tile, weights = first_ratings[:, cols], first_weights[:, cols]
                else:
                    tile, weights = ratings[0, stratum, :, cols], observed[0, stratum, :, cols]
                held = pieces[i]
                predicted = dot(current, held, ((1,), (1,)))
                residual = weights.astype(jnp.float32) * (tile - predicted)
                moved = held + step_rate * dot(residual, current, ((0,), (0,)))
                gained = step_rate * dot(residual, held, ((1,), (0,))) + gained
                gained = lax.optimization_barrier(gained)
                if stratum == last:
                    pieces[i] = home(moved, last, i in SPLIT_ROUTE)
                else:
                    pieces[i] = from_behind(moved, "users", -1)
            current = gained
        factors_u = combine(current)
    return (factors_u, jnp.concatenate(pieces, axis=0)[None])


def solution(mesh):
    in_specs = (
        P("period", None, "users", None),
        P("period", None, "users", None),
        P("users", None),
        P("period", "users", None),
    )
    out_specs = (P("users", None), P("period", "users", None))
    return jax.shard_map(
        on_device, mesh=mesh, in_specs=in_specs, out_specs=out_specs, check_vma=False
    )
```

```python
import functools

import jax
import jax.numpy as jnp
from jax import lax
from jax.experimental import pallas as pl
from jax.experimental.pallas import tpu as pltpu
from jax.sharding import PartitionSpec as P


OUTER = 2
STRATA = 3
PIECES = 3
LAYER = 4
FIRST_LEG = (4, 4, 4, 8)
SPLIT_ROUTE = (0,)


step_rate = 0.002


def from_behind(array, axis, by):
    peers = lax.axis_size(axis)
    return lax.ppermute(array, axis, [(i, (i + by) % peers) for i in range(peers)])


def home(array, by, split):
    peers = lax.axis_size("users")
    if not split or peers % LAYER:
        return from_behind(array, "users", by)
    legs = [FIRST_LEG[i % LAYER] for i in range(peers)]
    across = [(i, (i + leg) % peers) for i, leg in enumerate(legs)]
    within = [((i + leg) % peers, (i + by) % peers) for i, leg in enumerate(legs)]
    array = lax.ppermute(array, "users", across)
    return lax.ppermute(array, "users", within)


def dot(lhs, rhs, dims):
    return lax.dot_general(
        lhs, rhs, (dims, ((), ())), precision=lax.Precision.HIGH, preferred_element_type=jnp.float32
    )


def halves(x):
    high = x.astype(jnp.bfloat16)
    return high, (x - high.astype(jnp.float32)).astype(jnp.bfloat16)


def dot_of_halves(lhs, rhs, dims):
    part = functools.partial(
        lax.dot_general, dimension_numbers=(dims, ((), ())), preferred_element_type=jnp.float32
    )
    return part(lhs[0], rhs[0]) + (part(lhs[0], rhs[1]) + part(lhs[1], rhs[0]))


def first_kernel(c_in, v_in, r_in, w_in, c, v, r, w, residual, moved, sems):
    rows = moved.shape[0]
    start, rest = pl.ds(0, rows), pl.ds(rows, v.shape[0] - rows)
    copies = [
        pltpu.make_async_copy(source, target, sems.at[i])
        for i, (source, target) in enumerate(
            (
                (c_in, c),
                (v_in.at[0, start], v.at[start]),
                (r_in.at[0, 0, :, start], r.at[:, start]),
                (w_in.at[0, 0, :, start], w.at[:, start]),
                (v_in.at[0, rest], v.at[rest]),
                (r_in.at[0, 0, :, rest], r.at[:, rest]),
                (w_in.at[0, 0, :, rest], w.at[:, rest]),
            )
        )
    ]
    for copy in copies:
        copy.start()
    for copy in copies[:2]:
        copy.wait()
    c_halves = halves(c[...])
    predicted = dot_of_halves(c_halves, halves(v[start]), ((1,), (1,)))
    for copy in copies[2:4]:
        copy.wait()
    residual[...] = w[:, start].astype(jnp.float32) * (r[:, start] - predicted)
    change = dot_of_halves(halves(residual[...]), c_halves, ((0,), (0,)))
    moved[...] = v[start] + step_rate * change
    for copy in copies[4:]:
        copy.wait()


def first_piece(user_factors, item_factors, ratings, observed, rows):
    operands = (user_factors, item_factors, ratings, observed)
    users, rank = user_factors.shape
    outs = [
        jax.ShapeDtypeStruct(user_factors.shape, user_factors.dtype),
        jax.ShapeDtypeStruct(item_factors.shape[1:], item_factors.dtype),
        jax.ShapeDtypeStruct(ratings.shape[2:], ratings.dtype),
        jax.ShapeDtypeStruct(observed.shape[2:], observed.dtype),
        jax.ShapeDtypeStruct((users, rows), jnp.float32),
        jax.ShapeDtypeStruct((rows, rank), jnp.float32),
    ]
    return pl.pallas_call(
        first_kernel,
        out_shape=tuple(outs),
        in_specs=[pl.BlockSpec(memory_space=pltpu.HBM)] * 4,
        out_specs=(pl.BlockSpec(memory_space=pltpu.VMEM),) * len(outs),
        scratch_shapes=[pltpu.SemaphoreType.DMA((7,))],
        compiler_params=pltpu.CompilerParams(vmem_limit_bytes=16 << 20),
    )(*[pltpu.with_memory_space_constraint(a, pltpu.HBM) for a in operands])


def combine(current):
    periods_count = lax.axis_size("period")
    if periods_count & (periods_count - 1):
        summed = lax.psum(current, "period")
    else:
        summed, reach = current, 1
        while reach < periods_count:
            partners = [(i, i ^ reach) for i in range(periods_count)]
            partner = lax.ppermute(summed, "period", partners)
            summed = summed + partner
            reach *= 2
    return summed / periods_count


def on_device(ratings, observed, user_factors, item_factors):
    items = item_factors.shape[1]
    rows = items // PIECES
    factors_u, first_items, first_ratings, first_weights, *first = first_piece(
        user_factors, item_factors, ratings, observed, rows
    )
    pieces = [first_items[i * rows : (i + 1) * rows] for i in range(PIECES)]
    last = OUTER * STRATA - 1
    for outer_step in range(OUTER):
        current = factors_u
        for within in range(STRATA):
            stratum = outer_step * STRATA + within
            gained = current
            for i in range(PIECES):
                cols = slice(i * rows, (i + 1) * rows)
                if stratum == 0:
                    tile, weights = first_ratings[:, cols], first_weights[:, cols]
                else:
                    tile, weights = ratings[0, stratum, :, cols], observed[0, stratum, :, cols]
                held = pieces[i]
                if stratum == 0 and i == 0:
                    residual, moved = first
                else:
                    predicted = dot(current, held, ((1,), (1,)))
                    residual = weights.astype(jnp.float32) * (tile - predicted)
                    moved = held + step_rate * dot(residual, current, ((0,), (0,)))
                gained = step_rate * dot(residual, held, ((1,), (0,))) + gained
                gained = lax.optimization_barrier(gained)
                if stratum == last:
                    pieces[i] = home(moved, last, i in SPLIT_ROUTE)
                else:
                    pieces[i] = from_behind(moved, "users", -1)
            current = gained
        factors_u = combine(current)
    return (factors_u, jnp.concatenate(pieces, axis=0)[None])


def solution(mesh):
    in_specs = (
        P("period", None, "users", None),
        P("period", None, "users", None),
        P("users", None),
        P("period", "users", None),
    )
    out_specs = (P("users", None), P("period", "users", None))
    return jax.shard_map(
        on_device, mesh=mesh, in_specs=in_specs, out_specs=out_specs, check_vma=False
    )
```

```python
import functools

import jax
import jax.numpy as jnp
from jax import lax
from jax.experimental import pallas as pl
from jax.experimental.pallas import tpu as pltpu
from jax.sharding import PartitionSpec as P


OUTER = 2
STRATA = 3
PIECES = 3
LAYER = 4
FIRST_LEG = (4, 4, 4, 8)
SPLIT_ROUTE = (0,)


step_rate = 0.002


def from_behind(array, axis, by):
    peers = lax.axis_size(axis)
    return lax.ppermute(array, axis, [(i, (i + by) % peers) for i in range(peers)])


def home(array, by, split):
    peers = lax.axis_size("users")
    if not split or peers % LAYER:
        return from_behind(array, "users", by)
    legs = [FIRST_LEG[i % LAYER] for i in range(peers)]
    across = [(i, (i + leg) % peers) for i, leg in enumerate(legs)]
    within = [((i + leg) % peers, (i + by) % peers) for i, leg in enumerate(legs)]
    array = lax.ppermute(array, "users", across)
    return lax.ppermute(array, "users", within)


def dot(lhs, rhs, dims):
    return lax.dot_general(
        lhs, rhs, (dims, ((), ())), precision=lax.Precision.HIGH, preferred_element_type=jnp.float32
    )


def halves(x):
    high = x.astype(jnp.bfloat16)
    return high, (x - high.astype(jnp.float32)).astype(jnp.bfloat16)


def dot_of_halves(lhs, rhs, dims):
    return lax.dot_general(
        jnp.concatenate([lhs[0], lhs[0], lhs[1]], axis=dims[0][0]),
        jnp.concatenate([rhs[0], rhs[1], rhs[0]], axis=dims[1][0]),
        (dims, ((), ())),
        preferred_element_type=jnp.float32,
    )


def first_kernel(c_in, v_in, r_in, w_in, c, v, r, w, residual, moved, sems):
    rows = moved.shape[0]
    start, rest = pl.ds(0, rows), pl.ds(rows, v.shape[0] - rows)
    copies = [
        pltpu.make_async_copy(source, target, sems.at[i])
        for i, (source, target) in enumerate(
            (
                (c_in, c),
                (v_in.at[0, start], v.at[start]),
                (r_in.at[0, 0, :, start], r.at[:, start]),
                (w_in.at[0, 0, :, start], w.at[:, start]),
                (v_in.at[0, rest], v.at[rest]),
                (r_in.at[0, 0, :, rest], r.at[:, rest]),
                (w_in.at[0, 0, :, rest], w.at[:, rest]),
            )
        )
    ]
    for copy in copies:
        copy.start()
    for copy in copies[:2]:
        copy.wait()
    c_halves = halves(c[...])
    predicted = dot_of_halves(c_halves, halves(v[start]), ((1,), (1,)))
    for copy in copies[2:4]:
        copy.wait()
    residual[...] = w[:, start].astype(jnp.float32) * (r[:, start] - predicted)
    change = dot_of_halves(halves(residual[...]), c_halves, ((0,), (0,)))
    moved[...] = v[start] + step_rate * change
    for copy in copies[4:]:
        copy.wait()


def first_piece(user_factors, item_factors, ratings, observed, rows):
    operands = (user_factors, item_factors, ratings, observed)
    users, rank = user_factors.shape
    outs = [
        jax.ShapeDtypeStruct(user_factors.shape, user_factors.dtype),
        jax.ShapeDtypeStruct(item_factors.shape[1:], item_factors.dtype),
        jax.ShapeDtypeStruct(ratings.shape[2:], ratings.dtype),
        jax.ShapeDtypeStruct(observed.shape[2:], observed.dtype),
        jax.ShapeDtypeStruct((users, rows), jnp.float32),
        jax.ShapeDtypeStruct((rows, rank), jnp.float32),
    ]
    return pl.pallas_call(
        first_kernel,
        out_shape=tuple(outs),
        in_specs=[pl.BlockSpec(memory_space=pltpu.HBM)] * 4,
        out_specs=(pl.BlockSpec(memory_space=pltpu.VMEM),) * len(outs),
        scratch_shapes=[pltpu.SemaphoreType.DMA((7,))],
        compiler_params=pltpu.CompilerParams(vmem_limit_bytes=16 << 20),
    )(*[pltpu.with_memory_space_constraint(a, pltpu.HBM) for a in operands])


def store_kernel(spans, *refs):
    pieces, whole, sems = refs[: len(spans)], refs[-2], refs[-1]
    copies = [
        pltpu.make_async_copy(piece, whole.at[0, span], sems.at[i])
        for i, (piece, span) in enumerate(zip(pieces, spans))
    ]
    for copy in copies:
        copy.start()
    for copy in copies:
        copy.wait()


def store(pieces, spans, shape, whole=None):
    anywhere = pl.BlockSpec(memory_space=pltpu.HBM)
    inside = pl.BlockSpec(memory_space=pltpu.VMEM)
    return pl.pallas_call(
        functools.partial(store_kernel, spans),
        out_shape=jax.ShapeDtypeStruct(shape, jnp.float32),
        in_specs=[inside] * len(pieces) + [anywhere] * (whole is not None),
        out_specs=anywhere,
        input_output_aliases={} if whole is None else {len(pieces): 0},
        scratch_shapes=[pltpu.SemaphoreType.DMA((len(pieces),))],
        compiler_params=pltpu.CompilerParams(vmem_limit_bytes=8 << 20),
    )(*pieces, *([] if whole is None else [whole]))


def combine(current):
    periods_count = lax.axis_size("period")
    if periods_count & (periods_count - 1):
        summed = lax.psum(current, "period")
    else:
        summed, reach = current, 1
        while reach < periods_count:
            partners = [(i, i ^ reach) for i in range(periods_count)]
            partner = lax.ppermute(summed, "period", partners)
            summed = summed + partner
            reach *= 2
    return summed / periods_count


def on_device(ratings, observed, user_factors, item_factors):
    items = item_factors.shape[1]
    rows = items // PIECES
    factors_u, first_items, first_ratings, first_weights, *first = first_piece(
        user_factors, item_factors, ratings, observed, rows
    )
    pieces = [first_items[i * rows : (i + 1) * rows] for i in range(PIECES)]
    last = OUTER * STRATA - 1
    for outer_step in range(OUTER):
        current = factors_u
        for within in range(STRATA):
            stratum = outer_step * STRATA + within
            gained = current
            for i in range(PIECES):
                cols = slice(i * rows, (i + 1) * rows)
                if stratum == 0:
                    tile, weights = first_ratings[:, cols], first_weights[:, cols]
                else:
                    tile, weights = ratings[0, stratum, :, cols], observed[0, stratum, :, cols]
                held = pieces[i]
                if stratum == 0 and i == 0:
                    residual, moved = first
                else:
                    predicted = dot(current, held, ((1,), (1,)))
                    residual = weights.astype(jnp.float32) * (tile - predicted)
                    moved = held + step_rate * dot(residual, current, ((0,), (0,)))
                gained = step_rate * dot(residual, held, ((1,), (0,))) + gained
                gained = lax.optimization_barrier(gained)
                if stratum == last:
                    pieces[i] = home(moved, last, i in SPLIT_ROUTE)
                else:
                    pieces[i] = from_behind(moved, "users", -1)
            current = gained
        factors_u = combine(current)
    spans = tuple(slice(i * rows, (i + 1) * rows) for i in range(PIECES))
    whole = store(pieces[:-1], spans[:-1], item_factors.shape)
    return (factors_u, store(pieces[-1:], spans[-1:], item_factors.shape, whole))


def solution(mesh):
    in_specs = (
        P("period", None, "users", None),
        P("period", None, "users", None),
        P("users", None),
        P("period", "users", None),
    )
    out_specs = (P("users", None), P("period", "users", None))
    return jax.shard_map(
        on_device, mesh=mesh, in_specs=in_specs, out_specs=out_specs, check_vma=False
    )
```

```python
import jax
import jax.numpy as jnp
from jax import lax
from jax.experimental import pallas as pl
from jax.experimental.pallas import tpu as pltpu
from jax.sharding import PartitionSpec as P


OUTER = 2
STRATA = 3
PIECES = 3
LAYER = 4
FIRST_LEG = (4, 4, 4, 8)
SPLIT_ROUTE = (0,)


step_rate = 0.002


def from_behind(array, axis, by):
    peers = lax.axis_size(axis)
    return lax.ppermute(array, axis, [(i, (i + by) % peers) for i in range(peers)])


def home(array, by, split):
    peers = lax.axis_size("users")
    if not split or peers % LAYER:
        return from_behind(array, "users", by)
    legs = [FIRST_LEG[i % LAYER] for i in range(peers)]
    across = [(i, (i + leg) % peers) for i, leg in enumerate(legs)]
    within = [((i + leg) % peers, (i + by) % peers) for i, leg in enumerate(legs)]
    array = lax.ppermute(array, "users", across)
    return lax.ppermute(array, "users", within)


def dot(lhs, rhs, dims):
    return lax.dot_general(
        lhs, rhs, (dims, ((), ())), precision=lax.Precision.HIGH, preferred_element_type=jnp.float32
    )


def halves(x):
    high = x.astype(jnp.bfloat16)
    return high, (x - high.astype(jnp.float32)).astype(jnp.bfloat16)


def dot_of_halves(lhs, rhs, dims):
    return lax.dot_general(
        jnp.concatenate([lhs[0], lhs[0], lhs[1]], axis=dims[0][0]),
        jnp.concatenate([rhs[0], rhs[1], rhs[0]], axis=dims[1][0]),
        (dims, ((), ())),
        preferred_element_type=jnp.float32,
    )


def first_kernel(c_in, v_in, r_in, w_in, c, v, r, w, residual, moved, sems):
    rows = moved.shape[0]
    start, rest = pl.ds(0, rows), pl.ds(rows, v.shape[0] - rows)
    copies = [
        pltpu.make_async_copy(source, target, sems.at[i])
        for i, (source, target) in enumerate(
            (
                (c_in, c),
                (v_in.at[0, start], v.at[start]),
                (r_in.at[0, 0, :, start], r.at[:, start]),
                (w_in.at[0, 0, :, start], w.at[:, start]),
                (v_in.at[0, rest], v.at[rest]),
                (r_in.at[0, 0, :, rest], r.at[:, rest]),
                (w_in.at[0, 0, :, rest], w.at[:, rest]),
            )
        )
    ]
    for copy in copies:
        copy.start()
    for copy in copies[:2]:
        copy.wait()
    c_halves = halves(c[...])
    predicted = dot_of_halves(c_halves, halves(v[start]), ((1,), (1,)))
    for copy in copies[2:4]:
        copy.wait()
    residual[...] = w[:, start].astype(jnp.float32) * (r[:, start] - predicted)
    change = dot_of_halves(halves(residual[...]), c_halves, ((0,), (0,)))
    moved[...] = v[start] + step_rate * change
    for copy in copies[4:]:
        copy.wait()


def first_piece(user_factors, item_factors, ratings, observed, rows):
    operands = (user_factors, item_factors, ratings, observed)
    users, rank = user_factors.shape
    outs = [
        jax.ShapeDtypeStruct(user_factors.shape, user_factors.dtype),
        jax.ShapeDtypeStruct(item_factors.shape[1:], item_factors.dtype),
        jax.ShapeDtypeStruct(ratings.shape[2:], ratings.dtype),
        jax.ShapeDtypeStruct(observed.shape[2:], observed.dtype),
        jax.ShapeDtypeStruct((users, rows), jnp.float32),
        jax.ShapeDtypeStruct((rows, rank), jnp.float32),
    ]
    return pl.pallas_call(
        first_kernel,
        out_shape=tuple(outs),
        in_specs=[pl.BlockSpec(memory_space=pltpu.HBM)] * 4,
        out_specs=(pl.BlockSpec(memory_space=pltpu.VMEM),) * len(outs),
        scratch_shapes=[pltpu.SemaphoreType.DMA((7,))],
        compiler_params=pltpu.CompilerParams(vmem_limit_bytes=16 << 20),
    )(*[pltpu.with_memory_space_constraint(a, pltpu.HBM) for a in operands])


def combine(current):
    periods_count = lax.axis_size("period")
    if periods_count & (periods_count - 1):
        summed = lax.psum(current, "period")
    else:
        summed, reach = current, 1
        while reach < periods_count:
            partners = [(i, i ^ reach) for i in range(periods_count)]
            partner = lax.ppermute(summed, "period", partners)
            summed = summed + partner
            reach *= 2
    return summed / periods_count


def on_device(ratings, observed, user_factors, item_factors):
    items = item_factors.shape[1]
    rows = items // PIECES
    factors_u, first_items, first_ratings, first_weights, *first = first_piece(
        user_factors, item_factors, ratings, observed, rows
    )
    pieces = [first_items[i * rows : (i + 1) * rows] for i in range(PIECES)]
    last = OUTER * STRATA - 1
    for outer_step in range(OUTER):
        current = factors_u
        for within in range(STRATA):
            stratum = outer_step * STRATA + within
            gained = current
            for i in range(PIECES):
                cols = slice(i * rows, (i + 1) * rows)
                if stratum == 0:
                    tile, weights = first_ratings[:, cols], first_weights[:, cols]
                else:
                    tile, weights = ratings[0, stratum, :, cols], observed[0, stratum, :, cols]
                held = pieces[i]
                if stratum == 0 and i == 0:
                    residual, moved = first
                else:
                    predicted = dot(current, held, ((1,), (1,)))
                    residual = weights.astype(jnp.float32) * (tile - predicted)
                    moved = held + step_rate * dot(residual, current, ((0,), (0,)))
                gained = step_rate * dot(residual, held, ((1,), (0,))) + gained
                gained = lax.optimization_barrier(gained)
                if stratum == last:
                    pieces[i] = home(moved, last, i in SPLIT_ROUTE)
                else:
                    pieces[i] = from_behind(moved, "users", -1)
            current = gained
        factors_u = combine(current)
    return (factors_u, jnp.concatenate(pieces, axis=0)[None])


def solution(mesh):
    in_specs = (
        P("period", None, "users", None),
        P("period", None, "users", None),
        P("users", None),
        P("period", "users", None),
    )
    out_specs = (P("users", None), P("period", "users", None))
    return jax.shard_map(
        on_device, mesh=mesh, in_specs=in_specs, out_specs=out_specs, check_vma=False
    )
```
